32 devices in a mesh: dp: 16 (over z, y, x), section: 2 (over core).
Axes of the slice: x: 2, y: 2, z: 4, core: 2. Of those that a mesh axis runs over, the one named last changes fastest.
Arguments:
- acts: bfloat16 [2, 2, 2048, 2048], P('section', None, 'dp'), may hold values from -6 to 6
- cotan: bfloat16 [2, 2, 2048, 384], P('section', None, 'dp'), may hold values from -0.09375 to 0.09375
- counts: int32 [2, 2, 16, 1], P('section', None, 'dp'), may hold values from 32 to 128
- weight: float32 [2, 786432], P('section', 'dp'), may hold values from -4 to 4
- moment: float32 [2, 786432], P('section', 'dp'), may hold values from -4 to 4
- second: float32 [2, 786432], P('section', 'dp'), may hold values from 0.1 to 1
Outputs:
- new_weight: float32 [2, 786432], P('section', 'dp')
- new_moment: float32 [2, 786432], P('section', 'dp')
- new_second: float32 [2, 786432], P('section', 'dp')
The draws below stay inside these ranges and needn't reach their ends.
All inputs are finite; a program needn't handle non-finite values.
Results may differ from the reference program's by a relative error of at most 0.0003.
Values sent between devices are 32-bit elements; how exact they have to be, the bound alone decides.
A program may use at most 64 MiB of HBM per device.

```python
import math
import jax
import jax.numpy as jnp
from jax import lax

D = 2048
F = 384
CAP = 128
MICRO = 1
ROWS_ALL = 2048
SECTIONS = 2
FLAT = 786432
N_DP = 16


def set_ends(result, own_key, least, top_value):
    index_at = [jax.random.randint(jax.random.fold_in(own_key, axis), (), 0, length) for axis, length in enumerate(result.shape)]
    main_axis = result.shape.index(max(result.shape))
    neighbour = index_at[:main_axis] + [(index_at[main_axis] + 1) % result.shape[main_axis]] + index_at[main_axis + 1:]
    return result.at[tuple(index_at)].set(least).at[tuple(neighbour)].set(top_value)


def levels(own_key, shape, split, low, high):
    level = 1.0
    for axis_at, parts in split:
        heights = jax.random.uniform(jax.random.fold_in(jax.random.fold_in(own_key, 6), axis_at), (parts,), jnp.float32, low / len(split), high / len(split))
        level = level * jnp.repeat(jnp.exp(heights), shape[axis_at] // parts).reshape((-1,) + (1,) * (len(shape) - 1 - axis_at))
    return level


def normal_values(stream_key, extent, width, reach, pieces=(), held_as=jnp.bfloat16):
    drawn = jax.random.normal(stream_key, extent, jnp.float32) * width
    if len(pieces) > 0:
        drawn = levels(stream_key, extent, pieces, -0.22, 0.18) * drawn
    return jnp.clip(drawn, min=-reach, max=reach).astype(held_as)


def setup_inputs(seed: int = 0) -> dict:
    key_of = jax.random.split(jax.random.key(seed), 7)
    return {
        "acts": normal_values(key_of[0], (SECTIONS, 2, ROWS_ALL, D), 1.0, 6.0, ((0, 2), (2, 16))),
        "cotan": normal_values(key_of[1], (SECTIONS, 2, ROWS_ALL, F), (2 * ROWS_ALL) ** -0.5, 0.09375, ((0, 2), (2, 16))),
        "counts": set_ends(jax.random.randint(key_of[2], (SECTIONS, 2, N_DP, MICRO), CAP // 4, CAP + 1), jax.random.fold_in(key_of[2], 1), CAP // 4, CAP).astype(jnp.int32),
        "weight": normal_values(key_of[3], (SECTIONS, FLAT), 0.5, 4.0, ((0, 2), (1, 16)), jnp.float32),
        "moment": normal_values(key_of[4], (SECTIONS, FLAT), 0.5, 4.0, ((0, 2), (1, 16)), jnp.float32),
        "second": jnp.clip(jnp.exp(math.log(1.0) - 2.3025851 * jax.random.uniform(key_of[5], (SECTIONS, FLAT), jnp.float32) ** levels(key_of[5], (SECTIONS, FLAT), ((0, 2), (1, 16)), -0.2, 0.2)), 0.1, 1.0),
    }


def layer_grad(acts_dir, cotan_dir, live_dir):
    blocks_a = acts_dir.reshape(N_DP, -1, acts_dir.shape[-1])
    blocks_c = cotan_dir.reshape(N_DP, -1, cotan_dir.shape[-1])
    blocks_m = live_dir.reshape(N_DP, -1)

    def step(carry, item):
        block_a, block_c, block_m = item
        masked = block_c * block_m[:, None].astype(jnp.bfloat16)
        term = jnp.einsum('rd,rf->df', block_a.astype(jnp.float32), masked.astype(jnp.float32), precision=lax.Precision.HIGHEST)
        return (carry + term, None)
    start = jnp.zeros((acts_dir.shape[-1], cotan_dir.shape[-1]), jnp.float32)
    total, unused = lax.scan(step, start, (blocks_a, blocks_c, blocks_m))
    return total

def reference(acts, cotan, counts, weight, moment, second):
    slot = lax.broadcasted_iota(jnp.int32, (MICRO, CAP), 1)
    live = (slot[None, None, None] < counts[..., None]).reshape(SECTIONS, 2, ROWS_ALL)
    outs_w, outs_m, outs_v = ([], [], [])
    for layer in range(SECTIONS):
        other = SECTIONS - 1 - layer
        grad = layer_grad(acts[layer, 0], cotan[layer, 0], live[layer, 0]) + layer_grad(acts[other, 1], cotan[other, 1], live[other, 1])
        grad = grad.reshape(-1)
        new_m = 0.9 * moment[layer] + 0.1 * grad
        new_v = 0.95 * second[layer] + 0.05 * grad * grad
        corr_m = new_m / (1.0 - 0.9 ** 10)
        corr_v = new_v / (1.0 - 0.95 ** 10)
        new_w = weight[layer] - 0.01 * (corr_m / (jnp.sqrt(corr_v) + 1e-08) + 0.1 * weight[layer])
        outs_w.append(new_w)
        outs_m.append(new_m)
        outs_v.append(new_v)
    return (jnp.stack(outs_w), jnp.stack(outs_m), jnp.stack(outs_v))
```

```python
import functools
import jax
import jax.numpy as jnp
from jax import lax
from jax.experimental import pallas as pl
from jax.experimental.pallas import tpu as pltpu
from jax.sharding import PartitionSpec as P

LANES = 128
MESH = pl.DeviceIdType.MESH


def adamw_shard(grad, weight_now, moment_now, second_now):
    new_m = 0.9 * moment_now + 0.1 * grad
    new_v = 0.95 * second_now + 0.05 * grad * grad
    corr_m = new_m / (1.0 - 0.9**10)
    corr_v = new_v / (1.0 - 0.95**10)
    new_w = weight_now - 0.01 * (corr_m / (jnp.sqrt(corr_v) + 1e-08) + 0.1 * weight_now)
    return (new_w, new_m, new_v)


def dp_digits(mesh):
    size = mesh.shape["dp"]
    line = mesh.devices.reshape(size, -1)[:, 0]
    digits = []
    if hasattr(line[0], "coords"):
        for axis in range(3):
            at = [device.coords[axis] for device in line]
            if len(set(at)) > 1:
                digits.append((len(set(at)), next(j for j in range(size) if at[j] != at[0])))
    total = 1
    for count, stride in digits:
        total *= count
    if total != size:
        digits = [(size, 1)] if size > 1 else []
    digits.sort()
    return [(1, 1)] * (3 - len(digits)) + digits


def reduce_kernel(digits, micro, acts, cotan, counts, out, acts_out, cotan_out, acts_in, cotan_in, lhs, rhs, grad, got1, got2, got3,
                  part_send, part_recv, send1, recv1, send2, recv2, send3, recv3):
    sections = lax.axis_size("section")
    section = lax.axis_index("section")
    dp = lax.axis_index("dp")
    mirror = sections - 1 - section
    (count_a, stride_a), (count_b, stride_b), (count_c, stride_c) = digits

    def moved(step, digit):
        count, stride = digit
        mine = lax.rem(lax.div(dp, stride), count)
        return (lax.rem(mine + step, count) - mine) * stride

    peers = [(dp, mirror)]
    for digit in digits:
        peers += [(dp + moved(step, digit), section) for step in range(1, digit[0])]
    barrier = pltpu.get_barrier_semaphore()
    for peer in peers:
        pl.semaphore_signal(barrier, inc=1, device_id=peer, device_id_type=MESH)

    rows, depth = acts.shape[1], acts.shape[2]
    width = cotan.shape[2]
    slots = rows // micro

    def masked(k):
        pieces = []
        for b in range(micro):
            block = cotan[k, b * slots:(b + 1) * slots, :].astype(jnp.float32)
            place = lax.broadcasted_iota(jnp.int32, (slots, width), 0)
            pieces.append(jnp.where(place < counts[k, b], block, 0.0))
        return pieces[0] if micro == 1 else jnp.concatenate(pieces, axis=0)

    cotan_out[...] = masked(1)
    acts_out[...] = acts[1].astype(jnp.float32)
    pl.semaphore_wait(barrier, len(peers))

    def to_mirror(src, dst, at):
        return pltpu.make_async_remote_copy(
            src_ref=src, dst_ref=dst, send_sem=part_send.at[at], recv_sem=part_recv.at[at],
            device_id=(dp, mirror), device_id_type=MESH)

    exchange = [to_mirror(cotan_out, cotan_in, 0), to_mirror(acts_out, acts_in, 1)]
    for copy in exchange:
        copy.start()
    lhs[0:rows, :] = acts[0]
    rhs[0:rows, :] = masked(0).astype(jnp.bfloat16)
    for copy in exchange:
        copy.wait_recv()
    rhs[rows:2 * rows, :] = cotan_in[...].astype(jnp.bfloat16)
    lhs[rows:2 * rows, :] = acts_in[...].astype(jnp.bfloat16)

    per_row = width // LANES
    tile = 256
    for t in range(depth // tile):
        product = lax.dot_general(
            lhs[:, t * tile:(t + 1) * tile], rhs[...], (((0,), (0,)), ((), ())), preferred_element_type=jnp.float32)
        for c in range(per_row):
            grad[pl.ds(t * tile * per_row + c, tile, stride=per_row), :] = product[:, c * LANES:(c + 1) * LANES]

    shard_rows = out.shape[0]
    half = shard_rows // 2
    orders = ((digits[0], digits[1]), (digits[1], digits[0]))
    last = digits[2]

    def block(o, step1, step2, step3):
        first, second = orders[o]
        owner = dp + moved(step1, first) + moved(step2, second) + moved(step3, last)
        return grad.at[pl.ds(pl.multiple_of(owner * shard_rows + o * half, 8), half), :]

    def base1(o, step1, step2, step3):
        first, second = orders[o]
        return ((step1 - 1) * second[0] + step2) * last[0] + step3

    def stage1(o, step1, step2, step3):
        at = base1(o, step1, step2, step3)
        return pltpu.make_async_remote_copy(
            src_ref=block(o, step1, step2, step3), dst_ref=got1[o].at[at], send_sem=send1[o].at[at], recv_sem=recv1[o].at[at],
            device_id=(dp + moved(step1, orders[o][0]), section), device_id_type=MESH)

    def stage2(o, step2, step3):
        at = (step2 - 1) * last[0] + step3
        return pltpu.make_async_remote_copy(
            src_ref=block(o, 0, step2, step3), dst_ref=got2[o].at[at], send_sem=send2[o].at[at], recv_sem=recv2[o].at[at],
            device_id=(dp + moved(step2, orders[o][1]), section), device_id_type=MESH)

    def stage3(o, step3):
        at = step3 - 1
        return pltpu.make_async_remote_copy(
            src_ref=block(o, 0, 0, step3), dst_ref=got3[o].at[at], send_sem=send3[o].at[at], recv_sem=recv3[o].at[at],
            device_id=(dp + moved(step3, last), section), device_id_type=MESH)

    started = []

    def start(copy):
        copy.start()
        started.append(copy)

    def arrived1(o, step2, step3):
        total = block(o, 0, step2, step3)[...]
        for step1 in range(1, orders[o][0][0]):
            stage1(o, step1, step2, step3).wait_recv()
            total += got1[o][base1(o, step1, step2, step3)]
        return total

    def arrived2(o, step3):
        total = arrived1(o, 0, step3)
        for step2 in range(1, orders[o][1][0]):
            stage2(o, step2, step3).wait_recv()
            total += got2[o][(step2 - 1) * last[0] + step3]
        return total

    steps3 = sorted(range(1, last[0]), key=lambda step: -min(step, last[0] - step)) + [0]

    def send_forward(i):
        if i < len(steps3):
            for o in range(2):
                for step1 in range(1, orders[o][0][0]):
                    for step2 in range(1, orders[o][1][0]):
                        start(stage1(o, step1, step2, steps3[i]))

    def send_own(i):
        if i < len(steps3):
            for o in range(2):
                for step1 in range(1, orders[o][0][0]):
                    start(stage1(o, step1, 0, steps3[i]))

    def send_second(i):
        for o in range(2):
            for step2 in range(1, orders[o][1][0]):
                block(o, 0, step2, steps3[i])[...] = arrived1(o, step2, steps3[i])
                start(stage2(o, step2, steps3[i]))

    def send_third(i):
        for o in range(2):
            block(o, 0, 0, steps3[i])[...] = arrived2(o, steps3[i])
            start(stage3(o, steps3[i]))

    send_forward(0)
    send_own(0)
    send_forward(1)
    for i in range(len(steps3)):
        send_second(i)
        send_own(i + 1)
        send_forward(i + 2)
        if i >= 1:
            send_third(i - 1)
    for o in range(2):
        total = arrived2(o, 0)
        for step3 in range(1, last[0]):
            stage3(o, step3).wait_recv()
            total += got3[o][step3 - 1]
        out[o * half:(o + 1) * half, :] = total
    for copy in exchange + started:
        copy.wait_send()


def shards(digits, acts, cotan, counts, weight, moment, second):
    micro = counts.shape[3]
    rows, depth = acts.shape[2], acts.shape[3]
    width = cotan.shape[3]
    shard_rows = weight.shape[1] // LANES
    half = shard_rows // 2
    counts1 = [(first - 1) * other * digits[2][0] for first, other in ((digits[0][0], digits[1][0]), (digits[1][0], digits[0][0]))]
    counts2 = [(other - 1) * digits[2][0] for other in (digits[1][0], digits[0][0])]
    counts3 = [digits[2][0] - 1] * 2

    def buffers(sizes):
        return [pltpu.VMEM((max(size, 1), half, LANES), jnp.float32) for size in sizes]

    def semaphores(sizes):
        return [pltpu.SemaphoreType.DMA((max(size, 1),)) for size in sizes]

    vmem = pl.BlockSpec(memory_space=pltpu.VMEM)
    shard = pl.pallas_call(
        functools.partial(reduce_kernel, digits, micro),
        out_shape=jax.ShapeDtypeStruct((shard_rows, LANES), jnp.float32),
        in_specs=[vmem, vmem, pl.BlockSpec(memory_space=pltpu.SMEM)],
        out_specs=vmem,
        scratch_shapes=[
            pltpu.VMEM((rows, depth), jnp.float32),
            pltpu.VMEM((rows, width), jnp.float32),
            pltpu.VMEM((rows, depth), jnp.float32),
            pltpu.VMEM((rows, width), jnp.float32),
            pltpu.VMEM((2 * rows, depth), jnp.bfloat16),
            pltpu.VMEM((2 * rows, width), jnp.bfloat16),
            pltpu.VMEM((depth * width // LANES, LANES), jnp.float32),
            buffers(counts1), buffers(counts2), buffers(counts3),
            pltpu.SemaphoreType.DMA((2,)), pltpu.SemaphoreType.DMA((2,)),
            semaphores(counts1), semaphores(counts1), semaphores(counts2), semaphores(counts2),
            semaphores(counts3), semaphores(counts3),
        ],
        compiler_params=pltpu.CompilerParams(collective_id=0, has_side_effects=True),
        name="reduce_grad",
    )(acts[0], cotan[0], counts[0, :, 0, :])
    new_w, new_m, new_v = adamw_shard(shard.reshape(1, -1), weight, moment, second)
    return (new_w, new_m, new_v)


def solution(mesh):
    in_specs = (
        P("section", None, "dp", None),
        P("section", None, "dp", None),
        P("section", None, "dp", None),
        P("section", "dp"),
        P("section", "dp"),
        P("section", "dp"),
    )
    out_specs = (P("section", "dp"), P("section", "dp"), P("section", "dp"))
    body = functools.partial(shards, dp_digits(mesh))
    return jax.shard_map(body, mesh=mesh, in_specs=in_specs, out_specs=out_specs, check_vma=False)
```

```python
import functools
import jax
import jax.numpy as jnp
from jax import lax
from jax.experimental import pallas as pl
from jax.experimental.pallas import tpu as pltpu
from jax.sharding import PartitionSpec as P

LANES = 128
MESH = pl.DeviceIdType.MESH


def adamw_shard(grad, weight_now, moment_now, second_now):
    new_m = 0.9 * moment_now + 0.1 * grad
    new_v = 0.95 * second_now + 0.05 * grad * grad
    corr_m = new_m / (1.0 - 0.9**10)
    corr_v = new_v / (1.0 - 0.95**10)
    new_w = weight_now - 0.01 * (corr_m / (jnp.sqrt(corr_v) + 1e-08) + 0.1 * weight_now)
    return (new_w, new_m, new_v)


def adamw_kernel(grad, weight, moment, second, new_weight, new_moment, new_second):
    new_w, new_m, new_v = adamw_shard(grad[...], weight[...], moment[...], second[...])
    new_weight[...] = new_w
    new_moment[...] = new_m
    new_second[...] = new_v


def dp_digits(mesh):
    size = mesh.shape["dp"]
    line = mesh.devices.reshape(size, -1)[:, 0]
    digits = []
    if hasattr(line[0], "coords"):
        for axis in range(3):
            at = [device.coords[axis] for device in line]
            if len(set(at)) > 1:
                digits.append((len(set(at)), next(j for j in range(size) if at[j] != at[0])))
    total = 1
    for count, stride in digits:
        total *= count
    if total != size:
        digits = [(size, 1)] if size > 1 else []
    digits.sort()
    return [(1, 1)] * (3 - len(digits)) + digits


def reduce_kernel(digits, micro, pieces, acts, cotan, counts, out, acts_held, cotan_held, acts_out, cotan_out, acts_in, cotan_in, rhs,
                  grad, got1, got2, got3, load_sem, part_send, part_recv, send1, recv1, send2, recv2, send3, recv3):
    sections = lax.axis_size("section")
    section = lax.axis_index("section")
    dp = lax.axis_index("dp")
    mirror = sections - 1 - section

    def moved(step, digit):
        count, stride = digit
        mine = lax.rem(lax.div(dp, stride), count)
        return (lax.rem(mine + step, count) - mine) * stride

    peers = [(dp, mirror)]
    for digit in digits:
        peers += [(dp + moved(step, digit), section) for step in range(1, digit[0])]
    barrier = pltpu.get_barrier_semaphore()
    for peer in peers:
        pl.semaphore_signal(barrier, inc=1, device_id=peer, device_id_type=MESH)
    loads = [
        pltpu.make_async_copy(cotan, cotan_held, load_sem.at[0]),
        pltpu.make_async_copy(acts.at[1], acts_held.at[1], load_sem.at[1]),
        pltpu.make_async_copy(acts.at[0], acts_held.at[0], load_sem.at[2]),
    ]
    for load in loads:
        load.start()

    rows, depth = acts.shape[1], acts.shape[2]
    width = cotan.shape[2]
    slots = rows // micro
    shard_rows = out.shape[0]
    half = shard_rows // 2
    orders = ((digits[0], digits[1]), (digits[1], digits[0]))
    last = digits[2]
    per_row = width // LANES

    def masked(k):
        parts = []
        for b in range(micro):
            block = cotan_held[k, b * slots:(b + 1) * slots, :].astype(jnp.float32)
            place = lax.broadcasted_iota(jnp.int32, (slots, width), 0)
            parts.append(jnp.where(place < counts[b, k], block, 0.0))
        return parts[0] if micro == 1 else jnp.concatenate(parts, axis=0)

    steps3 = sorted(range(1, last[0]), key=lambda step: -min(step, last[0] - step)) + [0]
    piece = depth // pieces
    by_owner = pieces == lax.axis_size("dp")
    kinds = {"forward": [], "own": [], "mine": []}
    for step_a in range(digits[0][0]):
        for step_b in range(digits[1][0]):
            kind = "forward" if step_a and step_b else "own" if step_a or step_b else "mine"
            kinds[kind].append((step_a, step_b))
    groups = [("forward", 0), ("own", 0), ("forward", 1)]
    groups += [(kind, i) for i in range(len(steps3)) for kind in ("own", "forward", "mine") if (kind, i) not in groups]
    owners, group_of = [], {}
    for kind, i in groups:
        if i < len(steps3):
            group_of[kind, i] = range(len(owners), len(owners) + len(kinds[kind]))
            for step_a, step_b in kinds[kind]:
                owners.append(dp + moved(step_a, digits[0]) + moved(step_b, digits[1]) + moved(steps3[i], last))
    if not by_owner:
        owners = list(range(pieces))

    def columns(at):
        start = owners[at] * piece
        return pl.ds(start if isinstance(start, int) else pl.multiple_of(start, LANES), piece)

    def to_mirror(src, dst, at):
        return pltpu.make_async_remote_copy(
            src_ref=src, dst_ref=dst, send_sem=part_send.at[at], recv_sem=part_recv.at[at],
            device_id=(dp, mirror), device_id_type=MESH)

    exchange = [to_mirror(acts_out.at[at], acts_in.at[at], at) for at in range(pieces)]
    exchange.append(to_mirror(cotan_out, cotan_in, pieces))
    loads[0].wait()
    cotan_out[...] = masked(1)
    rhs[0:rows, :] = masked(0).astype(jnp.bfloat16)
    loads[1].wait()
    for at in range(pieces):
        acts_out[at] = acts_held[1, :, columns(at)].astype(jnp.float32)
    pl.semaphore_wait(barrier, len(peers))
    exchange[pieces].start()
    for copy in exchange[:pieces]:
        copy.start()
    loads[2].wait()
    exchange[pieces].wait_recv()
    rhs[rows:2 * rows, :] = cotan_in[...].astype(jnp.bfloat16)

    def make(at):
        exchange[at].wait_recv()
        lhs = jnp.concatenate([acts_held[0, :, columns(at)], acts_in[at].astype(jnp.bfloat16)], axis=0)
        product = lax.dot_general(lhs, rhs[...], (((0,), (0,)), ((), ())), preferred_element_type=jnp.float32)
        first = owners[at] * (piece * per_row)
        if not isinstance(first, int):
            first = pl.multiple_of(first, 8)
        for c in range(per_row):
            grad[pl.ds(first + c, piece, stride=per_row), :] = product[:, c * LANES:(c + 1) * LANES]

    def make_group(kind, i):
        if by_owner and (kind, i) in group_of:
            for at in group_of.pop((kind, i)):
                make(at)

    if not by_owner:
        for at in range(pieces):
            make(at)

    def block(o, step1, step2, step3):
        first, second = orders[o]
        owner = dp + moved(step1, first) + moved(step2, second) + moved(step3, last)
        return grad.at[pl.ds(pl.multiple_of(owner * shard_rows + o * half, 8), half), :]

    def base1(o, step1, step2, step3):
        first, second = orders[o]
        return ((step1 - 1) * second[0] + step2) * last[0] + step3

    def stage1(o, step1, step2, step3):
        at = base1(o, step1, step2, step3)
        return pltpu.make_async_remote_copy(
            src_ref=block(o, step1, step2, step3), dst_ref=got1[o].at[at], send_sem=send1[o].at[at], recv_sem=recv1[o].at[at],
            device_id=(dp + moved(step1, orders[o][0]), section), device_id_type=MESH)

    def stage2(o, step2, step3):
        at = (step2 - 1) * last[0] + step3
        return pltpu.make_async_remote_copy(
            src_ref=block(o, 0, step2, step3), dst_ref=got2[o].at[at], send_sem=send2[o].at[at], recv_sem=recv2[o].at[at],
            device_id=(dp + moved(step2, orders[o][1]), section), device_id_type=MESH)

    def stage3(o, step3):
        at = step3 - 1
        return pltpu.make_async_remote_copy(
            src_ref=block(o, 0, 0, step3), dst_ref=got3[o].at[at], send_sem=send3[o].at[at], recv_sem=recv3[o].at[at],
            device_id=(dp + moved(step3, last), section), device_id_type=MESH)

    started = []

    def start(copy):
        copy.start()
        started.append(copy)

    def arrived1(o, step2, step3):
        total = block(o, 0, step2, step3)[...]
        for step1 in range(1, orders[o][0][0]):
            stage1(o, step1, step2, step3).wait_recv()
            total += got1[o][base1(o, step1, step2, step3)]
        return total

    def arrived2(o, step3):
        total = arrived1(o, 0, step3)
        for step2 in range(1, orders[o][1][0]):
            stage2(o, step2, step3).wait_recv()
            total += got2[o][(step2 - 1) * last[0] + step3]
        return total

    def send_forward(i):
        if i < len(steps3):
            for o in range(2):
                for step1 in range(1, orders[o][0][0]):
                    for step2 in range(1, orders[o][1][0]):
                        start(stage1(o, step1, step2, steps3[i]))

    def send_own(i):
        if i < len(steps3):
            for o in range(2):
                for step1 in range(1, orders[o][0][0]):
                    start(stage1(o, step1, 0, steps3[i]))

    def send_second(i):
        for o in range(2):
            for step2 in range(1, orders[o][1][0]):
                block(o, 0, step2, steps3[i])[...] = arrived1(o, step2, steps3[i])
                start(stage2(o, step2, steps3[i]))

    def send_third(i):
        for o in range(2):
            block(o, 0, 0, steps3[i])[...] = arrived2(o, steps3[i])
            start(stage3(o, steps3[i]))

    make_group("forward", 0)
    send_forward(0)
    make_group("own", 0)
    send_own(0)
    make_group("forward", 1)
    send_forward(1)
    for kind, i in list(group_of):
        make_group(kind, i)
    for i in range(len(steps3)):
        send_second(i)
        send_own(i + 1)
        send_forward(i + 2)
        if i >= 1:
            send_third(i - 1)
    for o in range(2):
        total = arrived2(o, 0)
        for step3 in range(1, last[0]):
            stage3(o, step3).wait_recv()
            total += got3[o][step3 - 1]
        out[o * half:(o + 1) * half, :] = total
    for copy in exchange + started:
        copy.wait_send()


def shards(digits, acts, cotan, counts, weight, moment, second):
    micro = counts.shape[3]
    rows, depth = acts.shape[2], acts.shape[3]
    width = cotan.shape[3]
    shard_rows = weight.shape[1] // LANES
    half = shard_rows // 2
    piece = weight.shape[1] // width
    pieces = depth // piece if piece % LANES == 0 and weight.shape[1] % width == 0 else depth // (2 * LANES)
    counts1 = [(first - 1) * other * digits[2][0] for first, other in ((digits[0][0], digits[1][0]), (digits[1][0], digits[0][0]))]
    counts2 = [(other - 1) * digits[2][0] for other in (digits[1][0], digits[0][0])]
    counts3 = [digits[2][0] - 1] * 2

    def buffers(sizes):
        return [pltpu.VMEM((max(size, 1), half, LANES), jnp.float32) for size in sizes]

    def semaphores(sizes):
        return [pltpu.SemaphoreType.DMA((max(size, 1),)) for size in sizes]

    hbm = pl.BlockSpec(memory_space=pl.ANY)
    vmem = pl.BlockSpec(memory_space=pltpu.VMEM)
    shard = pl.pallas_call(
        functools.partial(reduce_kernel, digits, micro, pieces),
        out_shape=jax.ShapeDtypeStruct((shard_rows, LANES), jnp.float32),
        in_specs=[hbm, hbm, pl.BlockSpec(memory_space=pltpu.SMEM)],
        out_specs=vmem,
        scratch_shapes=[
            pltpu.VMEM((2, rows, depth), jnp.bfloat16),
            pltpu.VMEM((2, rows, width), jnp.bfloat16),
            pltpu.VMEM((pieces, rows, depth // pieces), jnp.float32),
            pltpu.VMEM((rows, width), jnp.float32),
            pltpu.VMEM((pieces, rows, depth // pieces), jnp.float32),
            pltpu.VMEM((rows, width), jnp.float32),
            pltpu.VMEM((2 * rows, width), jnp.bfloat16),
            pltpu.VMEM((depth * width // LANES, LANES), jnp.float32),
            buffers(counts1), buffers(counts2), buffers(counts3),
            pltpu.SemaphoreType.DMA((3,)), pltpu.SemaphoreType.DMA((pieces + 1,)), pltpu.SemaphoreType.DMA((pieces + 1,)),
            semaphores(counts1), semaphores(counts1), semaphores(counts2), semaphores(counts2),
            semaphores(counts3), semaphores(counts3),
        ],
        compiler_params=pltpu.CompilerParams(collective_id=0, has_side_effects=True),
        name="reduce_grad",
    )(acts[0], cotan[0], counts[0, :, 0, :].T)
    flat = jax.ShapeDtypeStruct((shard_rows, LANES), jnp.float32)
    outs = pl.pallas_call(
        adamw_kernel,
        out_shape=(flat, flat, flat),
        in_specs=[vmem] * 4,
        out_specs=(vmem, vmem, vmem),
        name="adamw",
    )(shard, *(array.reshape(shard_rows, LANES) for array in (weight, moment, second)))
    return tuple(array.reshape(weight.shape) for array in outs)


def solution(mesh):
    in_specs = (
        P("section", None, "dp", None),
        P("section", None, "dp", None),
        P("section", None, "dp", None),
        P("section", "dp"),
        P("section", "dp"),
        P("section", "dp"),
    )
    out_specs = (P("section", "dp"), P("section", "dp"), P("section", "dp"))
    body = functools.partial(shards, dp_digits(mesh))
    return jax.shard_map(body, mesh=mesh, in_specs=in_specs, out_specs=out_specs, check_vma=False)
```

```python
import functools
import jax
import jax.numpy as jnp
from jax import lax
from jax.experimental import pallas as pl
from jax.experimental.pallas import tpu as pltpu
from jax.sharding import PartitionSpec as P

LANES = 128
MESH = pl.DeviceIdType.MESH


def adamw_shard(grad, weight_now, moment_now, second_now):
    new_m = 0.9 * moment_now + 0.1 * grad
    new_v = 0.95 * second_now + 0.05 * grad * grad
    corr_m = new_m / (1.0 - 0.9**10)
    corr_v = new_v / (1.0 - 0.95**10)
    new_w = weight_now - 0.01 * (corr_m / (jnp.sqrt(corr_v) + 1e-08) + 0.1 * weight_now)
    return (new_w, new_m, new_v)


def adamw_kernel(grad, weight, moment, second, new_weight, new_moment, new_second):
    new_w, new_m, new_v = adamw_shard(grad[...], weight[...], moment[...], second[...])
    new_weight[...] = new_w
    new_moment[...] = new_m
    new_second[...] = new_v


def dp_digits(mesh):
    size = mesh.shape["dp"]
    line = mesh.devices.reshape(size, -1)[:, 0]
    digits = []
    if hasattr(line[0], "coords"):
        for axis in range(3):
            at = [device.coords[axis] for device in line]
            if len(set(at)) > 1:
                digits.append((len(set(at)), next(j for j in range(size) if at[j] != at[0])))
    total = 1
    for count, stride in digits:
        total *= count
    if total != size:
        digits = [(size, 1)] if size > 1 else []
    digits.sort()
    return [(1, 1)] * (3 - len(digits)) + digits


def axis_orders(digits):
    a, b, c = digits
    return [(a, b, c), (b, a, c), (c, a, b), (c, b, a)]


def row_spans(shard_rows):
    late = shard_rows // 128 * 8
    early = (shard_rows - 2 * late) // 2
    spans = [(0, early), (early, early), (2 * early, late), (2 * early + late, late)]
    return spans[:4 if late else 2]


def reduce_kernel(digits, micro, pieces, acts, cotan, counts, out, acts_held, cotan_held, acts_out, cotan_out, acts_in, cotan_in, rhs,
                  grad, got1, got2, got3, entered, load_sem, part_send, part_recv, send1, recv1, send2, recv2, send3, recv3):
    sections = lax.axis_size("section")
    section = lax.axis_index("section")
    dp = lax.axis_index("dp")
    mirror = sections - 1 - section

    def moved(step, digit):
        count, stride = digit
        mine = lax.rem(lax.div(dp, stride), count)
        return (lax.rem(mine + step, count) - mine) * stride

    length = digits[2][0]
    place_c = lax.rem(lax.div(dp, digits[2][1]), length)
    left, right = (dp - digits[2][1], section), (dp + digits[2][1], section)
    has_left, has_right = place_c > 0, place_c < length - 1
    peers = [(dp, mirror)]
    for digit in digits[:2]:
        peers += [(dp + moved(step, digit), section) for step in range(1, digit[0])]
    barrier = pltpu.get_barrier_semaphore()
    for peer in peers:
        pl.semaphore_signal(barrier, inc=1, device_id=peer, device_id_type=MESH)
    pl.when(has_left)(lambda: pl.semaphore_signal(barrier, inc=1, device_id=left, device_id_type=MESH))
    pl.when(has_right)(lambda: pl.semaphore_signal(barrier, inc=1, device_id=right, device_id_type=MESH))
    loads = [
        pltpu.make_async_copy(cotan, cotan_held, load_sem.at[0]),
        pltpu.make_async_copy(acts.at[1], acts_held.at[1], load_sem.at[1]),
        pltpu.make_async_copy(acts.at[0], acts_held.at[0], load_sem.at[2]),
    ]
    for load in loads:
        load.start()

    rows, depth = acts.shape[1], acts.shape[2]
    width = cotan.shape[2]
    slots = rows // micro
    shard_rows = out.shape[0]
    orders = axis_orders(digits)
    spans = row_spans(shard_rows)
    last = digits[2]
    per_row = width // LANES

    def masked(k):
        parts = []
        for b in range(micro):
            block = cotan_held[k, b * slots:(b + 1) * slots, :].astype(jnp.float32)
            place = lax.broadcasted_iota(jnp.int32, (slots, width), 0)
            parts.append(jnp.where(place < counts[b, k], block, 0.0))
        return parts[0] if micro == 1 else jnp.concatenate(parts, axis=0)

    steps3 = sorted(range(1, last[0]), key=lambda step: -min(step, last[0] - step)) + [0]
    piece = depth // pieces
    by_owner = pieces == lax.axis_size("dp")
    kinds = {"forward": [], "own": [], "mine": []}
    for step_a in range(digits[0][0]):
        for step_b in range(digits[1][0]):
            kind = "forward" if step_a and step_b else "own" if step_a or step_b else "mine"
            kinds[kind].append((step_a, step_b))
    groups = [("forward", 0), ("own", 0), ("forward", 1)]
    groups += [(kind, i) for i in range(len(steps3)) for kind in ("own", "forward", "mine") if (kind, i) not in groups]
    owners, group_of = [], {}
    for kind, i in groups:
        if i < len(steps3):
            group_of[kind, i] = range(len(owners), len(owners) + len(kinds[kind]))
            for step_a, step_b in kinds[kind]:
                owners.append(dp + moved(step_a, digits[0]) + moved(step_b, digits[1]) + moved(steps3[i], last))
    if not by_owner:
        owners = list(range(pieces))

    def columns(at):
        start = owners[at] * piece
        return pl.ds(start if isinstance(start, int) else pl.multiple_of(start, LANES), piece)

    def to_mirror(src, dst, at):
        return pltpu.make_async_remote_copy(
            src_ref=src, dst_ref=dst, send_sem=part_send.at[at], recv_sem=part_recv.at[at],
            device_id=(dp, mirror), device_id_type=MESH)

    exchange = [to_mirror(acts_out.at[at], acts_in.at[at], at) for at in range(pieces)]
    exchange.append(to_mirror(cotan_out, cotan_in, pieces))
    loads[0].wait()
    cotan_out[...] = masked(1)
    rhs[0:rows, :] = masked(0).astype(jnp.bfloat16)
    loads[1].wait()
    for at in range(pieces):
        acts_out[at] = acts_held[1, :, columns(at)].astype(jnp.float32)
    pl.semaphore_wait(barrier, len(peers) + has_left.astype(jnp.int32) + has_right.astype(jnp.int32))

    def tell_right():
        pl.semaphore_signal(entered.at[0], inc=1, device_id=right, device_id_type=MESH)

    def tell_left():
        pl.semaphore_signal(entered.at[1], inc=1, device_id=left, device_id_type=MESH)

    def hand_on():
        for k in range(1, length - 1):
            pl.when(place_c > k)(lambda: pl.semaphore_wait(entered.at[0], 1))
            pl.when(jnp.logical_and(place_c > k, has_right))(tell_right)
            pl.when(place_c < length - 1 - k)(lambda: pl.semaphore_wait(entered.at[1], 1))
            pl.when(jnp.logical_and(place_c < length - 1 - k, has_left))(tell_left)

    pl.when(jnp.logical_and(has_left, has_right))(tell_right)
    pl.when(jnp.logical_and(has_left, has_right))(tell_left)
    exchange[pieces].start()
    for copy in exchange[:pieces]:
        copy.start()
    loads[2].wait()
    exchange[pieces].wait_recv()
    rhs[rows:2 * rows, :] = cotan_in[...].astype(jnp.bfloat16)

    def make(at):
        exchange[at].wait_recv()
        lhs = jnp.concatenate([acts_held[0, :, columns(at)], acts_in[at].astype(jnp.bfloat16)], axis=0)
        product = lax.dot_general(lhs, rhs[...], (((0,), (0,)), ((), ())), preferred_element_type=jnp.float32)
        first = owners[at] * (piece * per_row)
        if not isinstance(first, int):
            first = pl.multiple_of(first, 8)
        for c in range(per_row):
            grad[pl.ds(first + c, piece, stride=per_row), :] = product[:, c * LANES:(c + 1) * LANES]

    def make_group(kind, i):
        if by_owner and (kind, i) in group_of:
            for at in group_of.pop((kind, i)):
                make(at)

    if not by_owner:
        for at in range(pieces):
            make(at)

    def block(o, step1, step2, step3):
        first, second, third = orders[o]
        owner = dp + moved(step1, first) + moved(step2, second) + moved(step3, third)
        return grad.at[pl.ds(pl.multiple_of(owner * shard_rows + spans[o][0], 8), spans[o][1]), :]

    def base1(o, step1, step2, step3):
        first, second, third = orders[o]
        return ((step1 - 1) * second[0] + step2) * third[0] + step3

    def stage1(o, step1, step2, step3):
        at = base1(o, step1, step2, step3)
        return pltpu.make_async_remote_copy(
            src_ref=block(o, step1, step2, step3), dst_ref=got1[o].at[at], send_sem=send1[o].at[at], recv_sem=recv1[o].at[at],
            device_id=(dp + moved(step1, orders[o][0]), section), device_id_type=MESH)

    def stage2(o, step2, step3):
        at = (step2 - 1) * orders[o][2][0] + step3
        return pltpu.make_async_remote_copy(
            src_ref=block(o, 0, step2, step3), dst_ref=got2[o].at[at], send_sem=send2[o].at[at], recv_sem=recv2[o].at[at],
            device_id=(dp + moved(step2, orders[o][1]), section), device_id_type=MESH)

    def stage3(o, step3):
        at = step3 - 1
        return pltpu.make_async_remote_copy(
            src_ref=block(o, 0, 0, step3), dst_ref=got3[o].at[at], send_sem=send3[o].at[at], recv_sem=recv3[o].at[at],
            device_id=(dp + moved(step3, orders[o][2]), section), device_id_type=MESH)

    started = []

    def start(copy):
        copy.start()
        started.append(copy)

    def arrived1(o, step2, step3):
        total = block(o, 0, step2, step3)[...]
        for step1 in range(1, orders[o][0][0]):
            stage1(o, step1, step2, step3).wait_recv()
            total += got1[o][base1(o, step1, step2, step3)]
        return total

    def arrived2(o, step3):
        total = arrived1(o, 0, step3)
        for step2 in range(1, orders[o][1][0]):
            stage2(o, step2, step3).wait_recv()
            total += got2[o][(step2 - 1) * orders[o][2][0] + step3]
        return total

    def send_forward(i):
        if i < len(steps3):
            for o in range(2):
                for step1 in range(1, orders[o][0][0]):
                    for step2 in range(1, orders[o][1][0]):
                        start(stage1(o, step1, step2, steps3[i]))

    def send_own(i):
        if i < len(steps3):
            for o in range(2):
                for step1 in range(1, orders[o][0][0]):
                    start(stage1(o, step1, 0, steps3[i]))

    def send_second(i):
        for o in range(2):
            for step2 in range(1, orders[o][1][0]):
                block(o, 0, step2, steps3[i])[...] = arrived1(o, step2, steps3[i])
                start(stage2(o, step2, steps3[i]))

    def send_third(i):
        for o in range(2):
            block(o, 0, 0, steps3[i])[...] = arrived2(o, steps3[i])
            start(stage3(o, steps3[i]))

    late = range(2, len(spans))

    def late_first():
        for o in late:
            for step1 in steps3[:-1]:
                for step2 in reversed(range(orders[o][1][0])):
                    for step3 in reversed(range(orders[o][2][0])):
                        start(stage1(o, step1, step2, step3))

    def late_second():
        for o in late:
            for step2 in range(1, orders[o][1][0]):
                for step3 in reversed(range(orders[o][2][0])):
                    block(o, 0, step2, step3)[...] = arrived1(o, step2, step3)
                    start(stage2(o, step2, step3))

    def late_third():
        for o in late:
            for step3 in range(1, orders[o][2][0]):
                block(o, 0, 0, step3)[...] = arrived2(o, step3)
                start(stage3(o, step3))

    make_group("forward", 0)
    send_forward(0)
    make_group("own", 0)
    send_own(0)
    make_group("forward", 1)
    send_forward(1)
    for kind, i in list(group_of):
        make_group(kind, i)
    hand_on()
    late_first()
    for i in range(len(steps3)):
        send_second(i)
        send_own(i + 1)
        send_forward(i + 2)
        if i >= 1:
            send_third(i - 1)
        if i == len(steps3) - 3:
            late_second()
        if i == len(steps3) - 2:
            late_third()
    if len(steps3) < 3:
        late_second()
    if len(steps3) < 2:
        late_third()
    for o in reversed(range(len(spans))):
        total = arrived2(o, 0)
        for step3 in range(1, orders[o][2][0]):
            stage3(o, step3).wait_recv()
            total += got3[o][step3 - 1]
        out[spans[o][0]:spans[o][0] + spans[o][1], :] = total
    for copy in exchange + started:
        copy.wait_send()


def shards(digits, acts, cotan, counts, weight, moment, second):
    micro = counts.shape[3]
    rows, depth = acts.shape[2], acts.shape[3]
    width = cotan.shape[3]
    shard_rows = weight.shape[1] // LANES
    piece = weight.shape[1] // width
    pieces = depth // piece if piece % LANES == 0 and weight.shape[1] % width == 0 else depth // (2 * LANES)
    orders = axis_orders(digits)
    spans = row_spans(shard_rows)
    orders = orders[:len(spans)]
    counts1 = [(first[0] - 1) * second[0] * third[0] for first, second, third in orders]
    counts2 = [(second[0] - 1) * third[0] for first, second, third in orders]
    counts3 = [third[0] - 1 for first, second, third in orders]

    def buffers(sizes):
        return [pltpu.VMEM((max(size, 1), span[1], LANES), jnp.float32) for size, span in zip(sizes, spans)]

    def semaphores(sizes):
        return [pltpu.SemaphoreType.DMA((max(size, 1),)) for size in sizes]

    hbm = pl.BlockSpec(memory_space=pl.ANY)
    vmem = pl.BlockSpec(memory_space=pltpu.VMEM)
    shard = pl.pallas_call(
        functools.partial(reduce_kernel, digits, micro, pieces),
        out_shape=jax.ShapeDtypeStruct((shard_rows, LANES), jnp.float32),
        in_specs=[hbm, hbm, pl.BlockSpec(memory_space=pltpu.SMEM)],
        out_specs=vmem,
        scratch_shapes=[
            pltpu.VMEM((2, rows, depth), jnp.bfloat16),
            pltpu.VMEM((2, rows, width), jnp.bfloat16),
            pltpu.VMEM((pieces, rows, depth // pieces), jnp.float32),
            pltpu.VMEM((rows, width), jnp.float32),
            pltpu.VMEM((pieces, rows, depth // pieces), jnp.float32),
            pltpu.VMEM((rows, width), jnp.float32),
            pltpu.VMEM((2 * rows, width), jnp.bfloat16),
            pltpu.VMEM((depth * width // LANES, LANES), jnp.float32),
            buffers(counts1), buffers(counts2), buffers(counts3),
            pltpu.SemaphoreType.REGULAR((2,)),
            pltpu.SemaphoreType.DMA((3,)), pltpu.SemaphoreType.DMA((pieces + 1,)), pltpu.SemaphoreType.DMA((pieces + 1,)),
            semaphores(counts1), semaphores(counts1), semaphores(counts2), semaphores(counts2),
            semaphores(counts3), semaphores(counts3),
        ],
        compiler_params=pltpu.CompilerParams(collective_id=0, has_side_effects=True),
        name="reduce_grad",
    )(acts[0], cotan[0], counts[0, :, 0, :].T)
    flat = jax.ShapeDtypeStruct((shard_rows, LANES), jnp.float32)
    outs = pl.pallas_call(
        adamw_kernel,
        out_shape=(flat, flat, flat),
        in_specs=[vmem] * 4,
        out_specs=(vmem, vmem, vmem),
        name="adamw",
    )(shard, *(array.reshape(shard_rows, LANES) for array in (weight, moment, second)))
    return tuple(array.reshape(weight.shape) for array in outs)


def solution(mesh):
    in_specs = (
        P("section", None, "dp", None),
        P("section", None, "dp", None),
        P("section", None, "dp", None),
        P("section", "dp"),
        P("section", "dp"),
        P("section", "dp"),
    )
    out_specs = (P("section", "dp"), P("section", "dp"), P("section", "dp"))
    body = functools.partial(shards, dp_digits(mesh))
    return jax.shard_map(body, mesh=mesh, in_specs=in_specs, out_specs=out_specs, check_vma=False)
```

```python
import functools
import jax
import jax.numpy as jnp
from jax import lax
from jax.experimental import pallas as pl
from jax.experimental.pallas import tpu as pltpu
from jax.sharding import PartitionSpec as P

LANES = 128
MESH = pl.DeviceIdType.MESH


def adamw_shard(grad, weight_now, moment_now, second_now):
    new_m = 0.9 * moment_now + 0.1 * grad
    new_v = 0.95 * second_now + 0.05 * grad * grad
    corr_m = new_m / (1.0 - 0.9**10)
    corr_v = new_v / (1.0 - 0.95**10)
    new_w = weight_now - 0.01 * (corr_m / (jnp.sqrt(corr_v) + 1e-08) + 0.1 * weight_now)
    return (new_w, new_m, new_v)


def adamw_kernel(grad, weight, moment, second, new_weight, new_moment, new_second):
    new_w, new_m, new_v = adamw_shard(grad[...], weight[...], moment[...], second[...])
    new_weight[...] = new_w
    new_moment[...] = new_m
    new_second[...] = new_v


def dp_digits(mesh):
    size = mesh.shape["dp"]
    line = mesh.devices.reshape(size, -1)[:, 0]
    digits = []
    if hasattr(line[0], "coords"):
        for axis in range(3):
            at = [device.coords[axis] for device in line]
            if len(set(at)) > 1:
                digits.append((len(set(at)), next(j for j in range(size) if at[j] != at[0])))
    total = 1
    for count, stride in digits:
        total *= count
    if total != size:
        digits = [(size, 1)] if size > 1 else []
    digits.sort()
    return [(1, 1)] * (3 - len(digits)) + digits


def axis_orders(digits):
    a, b, c = digits
    return [(a, b, c), (b, a, c), (c, a, b), (c, b, a)]


def row_spans(shard_rows):
    late = shard_rows // 128 * 8
    early = (shard_rows - 2 * late) // 2
    spans = [(0, early), (early, early), (2 * early, late), (2 * early + late, late)]
    return spans[:4 if late else 2]


def reduce_kernel(digits, micro, pieces, acts, cotan, counts, out, acts_held, cotan_held, acts_out, cotan_out, acts_in, cotan_in, rhs,
                  grad, got1, got2, got3, load_sem, part_send, part_recv, send1, recv1, send2, recv2, send3, recv3):
    sections = lax.axis_size("section")
    section = lax.axis_index("section")
    dp = lax.axis_index("dp")
    mirror = sections - 1 - section

    def moved(step, digit):
        count, stride = digit
        mine = lax.rem(lax.div(dp, stride), count)
        return (lax.rem(mine + step, count) - mine) * stride

    peers = [(dp, mirror)]
    for digit in digits:
        peers += [(dp + moved(step, digit), section) for step in range(1, digit[0])]
    barrier = pltpu.get_barrier_semaphore()
    for peer in peers:
        pl.semaphore_signal(barrier, inc=1, device_id=peer, device_id_type=MESH)
    loads = [
        pltpu.make_async_copy(cotan, cotan_held, load_sem.at[0]),
        pltpu.make_async_copy(acts.at[1], acts_held.at[1], load_sem.at[1]),
        pltpu.make_async_copy(acts.at[0], acts_held.at[0], load_sem.at[2]),
    ]
    for load in loads:
        load.start()

    rows, depth = acts.shape[1], acts.shape[2]
    width = cotan.shape[2]
    slots = rows // micro
    shard_rows = out.shape[0]
    orders = axis_orders(digits)
    spans = row_spans(shard_rows)
    last = digits[2]
    per_row = width // LANES

    def masked(k):
        parts = []
        for b in range(micro):
            block = cotan_held[k, b * slots:(b + 1) * slots, :].astype(jnp.float32)
            place = lax.broadcasted_iota(jnp.int32, (slots, width), 0)
            parts.append(jnp.where(place < counts[b, k], block, 0.0))
        return parts[0] if micro == 1 else jnp.concatenate(parts, axis=0)

    steps3 = sorted(range(1, last[0]), key=lambda step: -min(step, last[0] - step)) + [0]
    piece = depth // pieces
    by_owner = pieces == lax.axis_size("dp")
    kinds = {"forward": [], "own": [], "mine": []}
    for step_a in range(digits[0][0]):
        for step_b in range(digits[1][0]):
            kind = "forward" if step_a and step_b else "own" if step_a or step_b else "mine"
            kinds[kind].append((step_a, step_b))
    groups = [("forward", 0), ("own", 0), ("forward", 1)]
    groups += [(kind, i) for i in range(len(steps3)) for kind in ("own", "forward", "mine") if (kind, i) not in groups]
    owners, places, group_of = [], [], {}
    for kind, i in groups:
        if i < len(steps3):
            group_of[kind, i] = range(len(owners), len(owners) + len(kinds[kind]))
            for step_a, step_b in kinds[kind]:
                places.append((step_a, step_b, steps3[i]))
                owners.append(dp + moved(step_a, digits[0]) + moved(step_b, digits[1]) + moved(steps3[i], last))
    if not by_owner:
        owners = list(range(pieces))

    def columns(at):
        start = owners[at] * piece
        return pl.ds(start if isinstance(start, int) else pl.multiple_of(start, LANES), piece)

    def to_mirror(src, dst, at):
        return pltpu.make_async_remote_copy(
            src_ref=src, dst_ref=dst, send_sem=part_send.at[at], recv_sem=part_recv.at[at],
            device_id=(dp, mirror), device_id_type=MESH)

    exchange = [to_mirror(acts_out.at[at], acts_in.at[at], at) for at in range(pieces)]
    exchange.append(to_mirror(cotan_out, cotan_in, pieces))
    loads[0].wait()
    cotan_out[...] = masked(1)
    rhs[0:rows, :] = masked(0).astype(jnp.bfloat16)
    loads[1].wait()
    for at in range(pieces):
        acts_out[at] = acts_held[1, :, columns(at)].astype(jnp.float32)
    pl.semaphore_wait(barrier, len(peers))
    exchange[pieces].start()
    for copy in exchange[:pieces]:
        copy.start()
    loads[2].wait()
    exchange[pieces].wait_recv()
    rhs[rows:2 * rows, :] = cotan_in[...].astype(jnp.bfloat16)

    def make(at):
        exchange[at].wait_recv()
        lhs = jnp.concatenate([acts_held[0, :, columns(at)], acts_in[at].astype(jnp.bfloat16)], axis=0)
        product = lax.dot_general(lhs, rhs[...], (((0,), (0,)), ((), ())), preferred_element_type=jnp.float32)
        first = owners[at] * (piece * per_row)
        if not isinstance(first, int):
            first = pl.multiple_of(first, 8)
        for c in range(per_row):
            grad[pl.ds(first + c, piece, stride=per_row), :] = product[:, c * LANES:(c + 1) * LANES]

    def make_group(kind, i):
        if by_owner and (kind, i) in group_of:
            for at in group_of.pop((kind, i)):
                make(at)
                made.append(places[at])

    made = []
    if not by_owner:
        for at in range(pieces):
            make(at)
        made += places

    def block(o, step1, step2, step3):
        first, second, third = orders[o]
        owner = dp + moved(step1, first) + moved(step2, second) + moved(step3, third)
        return grad.at[pl.ds(pl.multiple_of(owner * shard_rows + spans[o][0], 8), spans[o][1]), :]

    def base1(o, step1, step2, step3):
        first, second, third = orders[o]
        return ((step1 - 1) * second[0] + step2) * third[0] + step3

    def stage1(o, step1, step2, step3):
        at = base1(o, step1, step2, step3)
        return pltpu.make_async_remote_copy(
            src_ref=block(o, step1, step2, step3), dst_ref=got1[o].at[at], send_sem=send1[o].at[at], recv_sem=recv1[o].at[at],
            device_id=(dp + moved(step1, orders[o][0]), section), device_id_type=MESH)

    def stage2(o, step2, step3):
        at = (step2 - 1) * orders[o][2][0] + step3
        return pltpu.make_async_remote_copy(
            src_ref=block(o, 0, step2, step3), dst_ref=got2[o].at[at], send_sem=send2[o].at[at], recv_sem=recv2[o].at[at],
            device_id=(dp + moved(step2, orders[o][1]), section), device_id_type=MESH)

    def stage3(o, step3):
        at = step3 - 1
        return pltpu.make_async_remote_copy(
            src_ref=block(o, 0, 0, step3), dst_ref=got3[o].at[at], send_sem=send3[o].at[at], recv_sem=recv3[o].at[at],
            device_id=(dp + moved(step3, orders[o][2]), section), device_id_type=MESH)

    started = []

    def start(copy):
        copy.start()
        started.append(copy)

    def arrived1(o, step2, step3):
        total = block(o, 0, step2, step3)[...]
        for step1 in range(1, orders[o][0][0]):
            stage1(o, step1, step2, step3).wait_recv()
            total += got1[o][base1(o, step1, step2, step3)]
        return total

    def arrived2(o, step3):
        total = arrived1(o, 0, step3)
        for step2 in range(1, orders[o][1][0]):
            stage2(o, step2, step3).wait_recv()
            total += got2[o][(step2 - 1) * orders[o][2][0] + step3]
        return total

    def send_forward(i):
        if i < len(steps3):
            for o in range(2):
                for step1 in range(1, orders[o][0][0]):
                    for step2 in range(1, orders[o][1][0]):
                        start(stage1(o, step1, step2, steps3[i]))

    def send_own(i):
        if i < len(steps3):
            for o in range(2):
                for step1 in range(1, orders[o][0][0]):
                    start(stage1(o, step1, 0, steps3[i]))

    def send_second(i):
        for o in range(2):
            for step2 in range(1, orders[o][1][0]):
                block(o, 0, step2, steps3[i])[...] = arrived1(o, step2, steps3[i])
                start(stage2(o, step2, steps3[i]))

    def send_third(i):
        for o in range(2):
            block(o, 0, 0, steps3[i])[...] = arrived2(o, steps3[i])
            start(stage3(o, steps3[i]))

    late = range(2, len(spans))

    def late_first(step2, step3, step1):
        for o in late:
            if step1:
                start(stage1(o, step1, *((step2, step3) if orders[o][1] is digits[0] else (step3, step2))))

    def late_second():
        for o in late:
            for step2 in range(1, orders[o][1][0]):
                for step3 in reversed(range(orders[o][2][0])):
                    block(o, 0, step2, step3)[...] = arrived1(o, step2, step3)
                    start(stage2(o, step2, step3))

    def late_third():
        for o in late:
            for step3 in range(1, orders[o][2][0]):
                block(o, 0, 0, step3)[...] = arrived2(o, step3)
                start(stage3(o, step3))

    def send_late():
        while made:
            late_first(*made.pop(0))

    end = len(steps3) - 1
    make_group("forward", 0)
    send_forward(0)
    make_group("own", 0)
    send_own(0)
    send_late()
    make_group("forward", 1)
    if end > 1:
        send_forward(1)
    send_late()
    for kind, i in list(group_of):
        make_group(kind, i)
        send_late()
    for i in range(end + 1):
        if i == end and i:
            send_third(i - 1)
        send_second(i)
        if i == end - 1:
            send_forward(end)
        send_own(i + 1)
        if i + 2 < end:
            send_forward(i + 2)
        if 1 <= i < end:
            send_third(i - 1)
        if i == end - 2:
            late_second()
        if i == end - 1:
            late_third()
    if len(steps3) < 3:
        late_second()
    if len(steps3) < 2:
        late_third()
    for o in reversed(range(len(spans))):
        total = arrived2(o, 0)
        for step3 in range(1, orders[o][2][0]):
            stage3(o, step3).wait_recv()
            total += got3[o][step3 - 1]
        out[spans[o][0]:spans[o][0] + spans[o][1], :] = total
    for copy in exchange + started:
        copy.wait_send()


def shards(digits, acts, cotan, counts, weight, moment, second):
    micro = counts.shape[3]
    rows, depth = acts.shape[2], acts.shape[3]
    width = cotan.shape[3]
    shard_rows = weight.shape[1] // LANES
    piece = weight.shape[1] // width
    pieces = depth // piece if piece % LANES == 0 and weight.shape[1] % width == 0 else depth // (2 * LANES)
    orders = axis_orders(digits)
    spans = row_spans(shard_rows)
    orders = orders[:len(spans)]
    counts1 = [(first[0] - 1) * second[0] * third[0] for first, second, third in orders]
    counts2 = [(second[0] - 1) * third[0] for first, second, third in orders]
    counts3 = [third[0] - 1 for first, second, third in orders]

    def buffers(sizes):
        return [pltpu.VMEM((max(size, 1), span[1], LANES), jnp.float32) for size, span in zip(sizes, spans)]

    def semaphores(sizes):
        return [pltpu.SemaphoreType.DMA((max(size, 1),)) for size in sizes]

    hbm = pl.BlockSpec(memory_space=pl.ANY)
    vmem = pl.BlockSpec(memory_space=pltpu.VMEM)
    shard = pl.pallas_call(
        functools.partial(reduce_kernel, digits, micro, pieces),
        out_shape=jax.ShapeDtypeStruct((shard_rows, LANES), jnp.float32),
        in_specs=[hbm, hbm, pl.BlockSpec(memory_space=pltpu.SMEM)],
        out_specs=vmem,
        scratch_shapes=[
            pltpu.VMEM((2, rows, depth), jnp.bfloat16),
            pltpu.VMEM((2, rows, width), jnp.bfloat16),
            pltpu.VMEM((pieces, rows, depth // pieces), jnp.float32),
            pltpu.VMEM((rows, width), jnp.float32),
            pltpu.VMEM((pieces, rows, depth // pieces), jnp.float32),
            pltpu.VMEM((rows, width), jnp.float32),
            pltpu.VMEM((2 * rows, width), jnp.bfloat16),
            pltpu.VMEM((depth * width // LANES, LANES), jnp.float32),
            buffers(counts1), buffers(counts2), buffers(counts3),
            pltpu.SemaphoreType.DMA((3,)), pltpu.SemaphoreType.DMA((pieces + 1,)), pltpu.SemaphoreType.DMA((pieces + 1,)),
            semaphores(counts1), semaphores(counts1), semaphores(counts2), semaphores(counts2),
            semaphores(counts3), semaphores(counts3),
        ],
        compiler_params=pltpu.CompilerParams(collective_id=0, has_side_effects=True),
        name="reduce_grad",
    )(acts[0], cotan[0], counts[0, :, 0, :].T)
    flat = jax.ShapeDtypeStruct((shard_rows, LANES), jnp.float32)
    outs = pl.pallas_call(
        adamw_kernel,
        out_shape=(flat, flat, flat),
        in_specs=[vmem] * 4,
        out_specs=(vmem, vmem, vmem),
        name="adamw",
    )(shard, *(array.reshape(shard_rows, LANES) for array in (weight, moment, second)))
    return tuple(array.reshape(weight.shape) for array in outs)


def solution(mesh):
    in_specs = (
        P("section", None, "dp", None),
        P("section", None, "dp", None),
        P("section", None, "dp", None),
        P("section", "dp"),
        P("section", "dp"),
        P("section", "dp"),
    )
    out_specs = (P("section", "dp"), P("section", "dp"), P("section", "dp"))
    body = functools.partial(shards, dp_digits(mesh))
    return jax.shard_map(body, mesh=mesh, in_specs=in_specs, out_specs=out_specs, check_vma=False)
```
